128 devices in a mesh: dp: 8 (over z, core), tensor: 16 (over x, y).
Axes of the slice: x: 4, y: 4, z: 4, core: 2. Of those that a mesh axis runs over, the one named last changes fastest.
Arguments:
- grad_codes: bfloat16 [8, 1024, 14, 1024], P(None, 'tensor', None, 'dp'), may hold values from -6 to 6
- grad_scales: bfloat16 [8, 1024, 14, 8], P(None, 'tensor', None, 'dp'), may hold values from 0.0099487305 to 0.19921875
- block_slot: int32 [112], replicated, may hold values from 0 to 111, as said below
- left_basis: bfloat16 [128, 1024, 1024], P(('dp', 'tensor')), may hold values from -0.1875 to 0.1875
- right_basis: bfloat16 [128, 1024, 1024], P(('dp', 'tensor')), may hold values from -0.1875 to 0.1875
- first_moment: bfloat16 [128, 1024, 1024], P(('dp', 'tensor')), may hold values from -0.119628906 to 0.119628906
- second_moment: bfloat16 [128, 1024, 1024], P(('dp', 'tensor')), may hold values from 9.9658966e-05 to 0.0099487305
- left_gram: bfloat16 [128, 1024, 1024], P(('dp', 'tensor')), may hold values from -0.59765625 to 0.59765625
- right_gram: bfloat16 [128, 1024, 1024], P(('dp', 'tensor')), may hold values from -0.59765625 to 0.59765625
Outputs:
- update: bfloat16 [8, 1024, 14, 1024], P(None, 'tensor', None, 'dp')
- first_moment_new: bfloat16 [128, 1024, 1024], P(('dp', 'tensor'))
- second_moment_new: bfloat16 [128, 1024, 1024], P(('dp', 'tensor'))
- left_gram_new: bfloat16 [128, 1024, 1024], P(('dp', 'tensor'))
- right_gram_new: bfloat16 [128, 1024, 1024], P(('dp', 'tensor'))
The draws below stay inside these ranges and needn't reach their ends.
Inputs may be any that keep to these rules, and one draw needn't show every extreme that they name: `block_slot`: entries are distinct. Blocks are taken in an order drawn from the seed; the i-th goes to owner i mod 128, in its local slot i div 128, that is global slot (i mod 128) + i div 128.
All inputs are finite; a program needn't handle non-finite values.
Results may differ from the reference program's by a relative error of at most 0.0065.
Values may be sent and summed in bfloat16 or wider, within the bound.
A program may use at most 128 MiB of HBM per device.

```python
import math
import jax
import jax.numpy as jnp
from jax import lax

BS = 1024
GROUP = 128
NBR = 8
NBC = 14
NBLK = 112
OWNERS = 128
SLOTS = 1


def draw_block_slot(key, part):
    order = jax.random.permutation(jax.random.fold_in(key, 7), NBLK)
    position = jnp.arange(NBLK, dtype=jnp.int32)
    target = position % OWNERS * SLOTS + position // OWNERS
    return jnp.zeros((NBLK,), jnp.int32).at[order].set(target.astype(jnp.int32))


def steps_of(own_key, extent, split, least, high):
    loudness = 1.0
    for axis_at, blocks in split:
        heights = jax.random.uniform(jax.random.fold_in(jax.random.fold_in(own_key, 6), axis_at), (blocks,), jnp.float32, least / len(split), high / len(split))
        loudness = loudness * jnp.repeat(jnp.exp(heights), extent[axis_at] // blocks).reshape((-1,) + (1,) * (len(extent) - 1 - axis_at))
    return loudness


def bell_draw(stream_key, shape, scale, bound, cuts=(), kind=jnp.bfloat16):
    result = jax.random.normal(stream_key, shape, jnp.float32) * scale
    if len(cuts) > 0:
        result = steps_of(stream_key, shape, cuts, -0.22, 0.18) * result
    return jnp.clip(result, min=-bound, max=bound).astype(kind)


def setup_inputs(seed: int = 0) -> dict:
    arg_keys = jax.random.split(jax.random.key(seed), 10)
    grad_codes = bell_draw(arg_keys[0], (NBR, BS, NBC, BS), 1.0, 6.0, ((1, 16), (3, 8)))
    grad_scales = jnp.clip(jnp.exp(math.log(0.19921875) - 2.9969585 * jax.random.uniform(arg_keys[1], (NBR, BS, NBC, BS // GROUP), jnp.float32) ** steps_of(arg_keys[1], (NBR, BS, NBC, BS // GROUP), ((1, 16), (3, 8)), -0.2, 0.2)), 0.0099487305, 0.19921875).astype(jnp.bfloat16)
    block_slot = draw_block_slot(jax.random.fold_in(arg_keys[9], 71), 0)
    left_basis = bell_draw(arg_keys[3], (OWNERS * SLOTS, BS, BS), BS ** -0.5, 0.1875, ((0, 128),))
    right_basis = bell_draw(arg_keys[4], (OWNERS * SLOTS, BS, BS), BS ** -0.5, 0.1875, ((0, 128),))
    first_moment = bell_draw(arg_keys[5], (OWNERS * SLOTS, BS, BS), 0.02, 0.119628906, ((0, 128),))
    second_moment = jnp.clip(jnp.exp(math.log(0.0099487305) - 4.603446 * jax.random.uniform(arg_keys[6], (OWNERS * SLOTS, BS, BS), jnp.float32) ** steps_of(arg_keys[6], (OWNERS * SLOTS, BS, BS), ((0, 128),), -0.2, 0.2)), 9.965896606445312e-05, 0.0099487305).astype(jnp.bfloat16)
    left_gram = bell_draw(arg_keys[7], (OWNERS * SLOTS, BS, BS), 0.1, 0.59765625, ((0, 128),))
    right_gram = bell_draw(arg_keys[8], (OWNERS * SLOTS, BS, BS), 0.1, 0.59765625, ((0, 128),))
    return dict(grad_codes=grad_codes, grad_scales=grad_scales, block_slot=block_slot, left_basis=left_basis, right_basis=right_basis, first_moment=first_moment, second_moment=second_moment, left_gram=left_gram, right_gram=right_gram)


beta_first = 0.9
beta_second = 0.95
gram_decay = 0.9
epsilon = 1e-08

def soap_block(gradient, left_basis, right_basis, first_moment, second_moment, left_gram, right_gram):
    half = jnp.dot(left_basis.T, gradient, preferred_element_type=jnp.float32).astype(jnp.bfloat16)
    rotated = jnp.dot(half, right_basis, preferred_element_type=jnp.float32)
    moment_one = beta_first * first_moment.astype(jnp.float32) + (1.0 - beta_first) * rotated
    moment_two = beta_second * second_moment.astype(jnp.float32) + (1.0 - beta_second) * rotated * rotated
    direction = (moment_one / (jnp.sqrt(moment_two) + epsilon)).astype(jnp.bfloat16)
    half_back = jnp.dot(left_basis, direction, preferred_element_type=jnp.float32).astype(jnp.bfloat16)
    back = jnp.dot(half_back, right_basis.T, preferred_element_type=jnp.float32)
    left_new = gram_decay * left_gram.astype(jnp.float32) + (1.0 - gram_decay) * jnp.dot(gradient, gradient.T, preferred_element_type=jnp.float32)
    right_new = gram_decay * right_gram.astype(jnp.float32) + (1.0 - gram_decay) * jnp.dot(gradient.T, gradient, preferred_element_type=jnp.float32)
    return (back.astype(jnp.bfloat16), moment_one.astype(jnp.bfloat16), moment_two.astype(jnp.bfloat16), left_new.astype(jnp.bfloat16), right_new.astype(jnp.bfloat16))

def reference(grad_codes, grad_scales, block_slot, left_basis, right_basis, first_moment, second_moment, left_gram, right_gram):
    grouped = grad_codes.astype(jnp.float32).reshape(NBR, BS, NBC, BS // GROUP, GROUP)
    values = (grouped * grad_scales.astype(jnp.float32)[..., None]).reshape(NBR, BS, NBC, BS)
    blocks = values.transpose(0, 2, 1, 3).reshape(NBLK, BS, BS)
    slot_total = OWNERS * SLOTS
    holder = jnp.zeros((slot_total,), jnp.int32).at[block_slot].set(jnp.arange(NBLK, dtype=jnp.int32) + 1)

    def one_slot(position):
        block_index = holder[position]
        present = (block_index > 0).astype(jnp.float32)
        gradient = (blocks[jnp.maximum(block_index - 1, 0)] * present).astype(jnp.bfloat16)
        return soap_block(gradient, left_basis[position], right_basis[position], first_moment[position], second_moment[position], left_gram[position], right_gram[position])
    back, moment_one, moment_two, left_new, right_new = lax.map(one_slot, jnp.arange(slot_total, dtype=jnp.int32))
    placed = back[block_slot].reshape(NBR, NBC, BS, BS).transpose(0, 2, 1, 3)
    return (placed, moment_one, moment_two, left_new, right_new)
```

```python
import functools

import jax
import jax.numpy as jnp
from jax import lax
from jax.experimental import pallas as pl
from jax.experimental.pallas import tpu as pltpu
from jax.sharding import PartitionSpec as P

beta_first = 0.9
beta_second = 0.95
gram_decay = 0.9
epsilon = 1e-08

CHUNK = 256
SLICE = 16


def nt(a, b):
    return lax.dot_general(a, b, (((1,), (1,)), ((), ())), preferred_element_type=jnp.float32)


def nn(a, b):
    return jnp.dot(a, b, preferred_element_type=jnp.float32)


def digits(i, *sizes):
    out = []
    for n in sizes:
        out.append(lax.rem(i, n))
        i = i // n
    return out


def kernel(
    inverse,
    slots,
    codes_hbm,
    scales,
    left_hbm,
    right_hbm,
    first_hbm,
    second_hbm,
    lgram_hbm,
    rgram_hbm,
    update_out,
    first_out,
    second_out,
    lgram_out,
    rgram_out,
    codes,
    stage,
    grad,
    flip,
    left,
    left_t,
    right,
    first,
    second,
    lgram,
    rgram,
    half,
    rotated,
    direction,
    back,
    arrived,
    load_sem,
    out_sem,
    grad_send,
    grad_recv,
    back_send,
    back_recv,
):
    blocks, tile_rows, tile_cols = codes.shape
    side = grad.shape[0]
    dp_index = lax.axis_index("dp")
    t_index = lax.axis_index("tensor")
    z, c = dp_index // 2, lax.rem(dp_index, 2)
    x, y = t_index // 4, lax.rem(t_index, 4)
    me = dp_index * 16 + t_index
    owner = me < blocks

    barrier = pltpu.get_barrier_semaphore()

    @pl.loop(1, 128)
    def _(i):
        o = lax.rem(me + i, 128)
        pl.semaphore_signal(
            barrier, inc=1, device_id={"dp": o // 16, "tensor": lax.rem(o, 16)}
        )

    loads = [
        pltpu.make_async_copy(src, dst, load_sem.at[n])
        for n, (src, dst) in enumerate(
            (
                (codes_hbm, codes),
                (left_hbm, left),
                (right_hbm, right),
                (first_hbm, first),
                (second_hbm, second),
                (lgram_hbm, lgram),
                (rgram_hbm, rgram),
            )
        )
    ]
    for copy in loads:
        copy.start()

    eye = (
        lax.broadcasted_iota(jnp.int32, (tile_rows, tile_rows), 0)
        == lax.broadcasted_iota(jnp.int32, (tile_rows, tile_rows), 1)
    ).astype(jnp.bfloat16)
    scale_t = nt(eye, scales[...])
    lane = lax.broadcasted_iota(jnp.int32, (tile_rows, blocks), 1)
    lane_block = lax.rem(lane, 8) * 14 + lane // 8

    def tile_at(ref, o):
        rows = pl.multiple_of(lax.rem(o, 16) * tile_rows, tile_rows)
        cols = pl.multiple_of((o // 16) * tile_cols, tile_cols)
        return ref.at[pl.ds(rows, tile_rows), pl.ds(cols, tile_cols)]

    loads[0].wait()
    pl.semaphore_wait(barrier, 127)

    @pl.loop(0, 128)
    def _(i):
        dzb, a, b, zp, core = digits(i, 2, 4, 4, 2, 2)
        z2 = lax.rem(z + 2 * dzb + 1 - zp, 4)
        x2 = lax.rem(x + a, 4)
        y2 = lax.rem(y + a + b, 4)
        o = (z2 * 2 + core) * 16 + x2 * 4 + y2

        @pl.when(o < blocks)
        def _():
            block = inverse[o]
            scale = jnp.sum(
                jnp.where(lane_block == block, scale_t, 0.0), axis=1, keepdims=True
            )
            stage[o] = (codes[block].astype(jnp.float32) * scale).astype(jnp.bfloat16)

            @pl.when(o != me)
            def _():
                pltpu.make_async_remote_copy(
                    stage.at[o],
                    tile_at(grad, me),
                    grad_send,
                    grad_recv,
                    device_id={"dp": z2 * 2 + core, "tensor": x2 * 4 + y2},
                ).start()

    @pl.when(owner)
    def _():
        pltpu.sync_copy(stage.at[me], tile_at(grad, me))

    @pl.when(jnp.logical_not(owner))
    def _():
        grad[...] = jnp.zeros_like(grad)

    def chunked(body):
        @pl.loop(0, side // CHUNK)
        def _(i):
            body(pl.ds(pl.multiple_of(i * CHUNK, CHUNK), CHUNK))

    loads[1].wait()

    def flip_left(rows):
        left_t[rows, :] = left[:, rows].T

    chunked(flip_left)
    for copy in loads[2:]:
        copy.wait()

    @pl.when(owner)
    def _():
        pltpu.make_async_copy(
            arrived_bytes(arrived, 127), arrived_bytes(arrived, 127), grad_recv
        ).wait()

    def to_direction(rows):
        half_rows = nn(left_t[rows, :], grad[...]).astype(jnp.bfloat16)
        rotated[...] = nn(half_rows, right[...])

        @pl.loop(0, CHUNK // SLICE)
        def _(j):
            inner = pl.ds(pl.multiple_of(j * SLICE, SLICE), SLICE)
            outer = pl.ds(pl.multiple_of(rows.start + j * SLICE, SLICE), SLICE)
            turned = rotated[inner, :]
            m = beta_first * first[outer, :].astype(jnp.float32) + (1.0 - beta_first) * turned
            v = (
                beta_second * second[outer, :].astype(jnp.float32)
                + (1.0 - beta_second) * turned * turned
            )
            direction[outer, :] = (m / (jnp.sqrt(v) + epsilon)).astype(jnp.bfloat16)
            first[outer, :] = m.astype(jnp.bfloat16)
            second[outer, :] = v.astype(jnp.bfloat16)

    chunked(to_direction)
    stores = [
        pltpu.make_async_copy(first, first_out, out_sem.at[0]),
        pltpu.make_async_copy(second, second_out, out_sem.at[1]),
        pltpu.make_async_copy(lgram, lgram_out, out_sem.at[2]),
        pltpu.make_async_copy(rgram, rgram_out, out_sem.at[3]),
        pltpu.make_async_copy(codes, update_out, out_sem.at[4]),
    ]
    stores[0].start()
    stores[1].start()

    for parity in (1, 0):

        @pl.loop(0, 2)
        def _(k):
            x2 = lax.rem(x + 2 * k + parity, 4)
            rows = pl.ds(pl.multiple_of(x2 * CHUNK, CHUNK), CHUNK)
            half[...] = nn(left[rows, :], direction[...]).astype(jnp.bfloat16)
            back[rows, :] = nt(half[...], right[...]).astype(jnp.bfloat16)

        @pl.when(owner)
        def _():
            @pl.loop(0, 64)
            def _(i):
                dzb, k, dyb, core, zp, yp = digits(i, 2, 2, 2, 2, 2, 2)
                z2 = lax.rem(z + 2 * dzb + 1 - zp, 4)
                x2 = lax.rem(x + 2 * k + parity, 4)
                y2 = lax.rem(y + 2 * dyb + yp, 4)
                o = (z2 * 2 + core) * 16 + x2 * 4 + y2

                @pl.when(o != me)
                def _():
                    pltpu.make_async_remote_copy(
                        tile_at(back, o),
                        arrived.at[me],
                        back_send,
                        back_recv,
                        device_id={"dp": z2 * 2 + core, "tensor": x2 * 4 + y2},
                    ).start()

    @pl.when(owner)
    def _():
        pltpu.sync_copy(tile_at(back, me), arrived.at[me])

    def flip_grad(rows):
        flip[rows, :] = grad[:, rows].T

    chunked(flip_grad)

    def grams(rows):
        lgram[rows, :] = (
            gram_decay * lgram[rows, :].astype(jnp.float32)
            + (1.0 - gram_decay) * nt(grad[rows, :], grad[...])
        ).astype(jnp.bfloat16)
        rgram[rows, :] = (
            gram_decay * rgram[rows, :].astype(jnp.float32)
            + (1.0 - gram_decay) * nt(flip[rows, :], flip[...])
        ).astype(jnp.bfloat16)

    chunked(grams)
    stores[2].start()
    stores[3].start()

    @pl.when(owner)
    def _():
        pltpu.make_async_copy(
            arrived_bytes(arrived, 111), arrived_bytes(arrived, 111), back_recv
        ).wait()

    @pl.when(jnp.logical_not(owner))
    def _():
        pltpu.make_async_copy(
            arrived_bytes(arrived, 112), arrived_bytes(arrived, 112), back_recv
        ).wait()

    @pl.loop(0, blocks)
    def _(b):
        codes[b] = arrived[slots[b]]

    stores[4].start()

    @pl.when(owner)
    def _():
        pltpu.make_async_copy(
            arrived_bytes(arrived, 111), arrived_bytes(arrived, 111), grad_send
        ).wait()
        pltpu.make_async_copy(
            arrived_bytes(arrived, 127), arrived_bytes(arrived, 127), back_send
        ).wait()

    @pl.when(jnp.logical_not(owner))
    def _():
        pltpu.make_async_copy(
            arrived_bytes(arrived, 112), arrived_bytes(arrived, 112), grad_send
        ).wait()

    for copy in stores:
        copy.wait()


def arrived_bytes(ref, tiles):
    return ref.at[pl.ds(0, tiles)]


def on_device(
    grad_codes,
    grad_scales,
    block_slot,
    left_basis,
    right_basis,
    first_moment,
    second_moment,
    left_gram,
    right_gram,
):
    block_rows, tile_rows, block_cols, tile_cols = grad_codes.shape
    blocks = block_rows * block_cols
    side = left_basis.shape[1]
    bf16 = jnp.bfloat16
    order = jnp.arange(blocks, dtype=jnp.int32)
    inverse = jnp.sum(
        jnp.where(block_slot[None, :] == order[:, None], order[None, :], 0), axis=1
    )
    codes = grad_codes.transpose(0, 2, 1, 3).reshape(blocks, tile_rows, tile_cols)
    scales = grad_scales.transpose(2, 3, 0, 1).reshape(blocks, tile_rows)
    square = (side, side)
    anywhere = pl.BlockSpec(memory_space=pl.ANY)
    outs = pl.pallas_call(
        kernel,
        name="soap_exchange",
        out_shape=[jax.ShapeDtypeStruct((blocks, tile_rows, tile_cols), bf16)]
        + [jax.ShapeDtypeStruct(square, bf16)] * 4,
        in_specs=[
            pl.BlockSpec(memory_space=pltpu.SMEM),
            pl.BlockSpec(memory_space=pltpu.SMEM),
            anywhere,
            pl.BlockSpec(memory_space=pltpu.VMEM),
        ]
        + [anywhere] * 6,
        out_specs=[anywhere] * 5,
        scratch_shapes=[
            pltpu.VMEM((blocks, tile_rows, tile_cols), bf16),
            pltpu.VMEM((blocks, tile_rows, tile_cols), bf16),
        ]
        + [pltpu.VMEM(square, bf16)] * 9
        + [
            pltpu.VMEM((CHUNK, side), bf16),
            pltpu.VMEM((CHUNK, side), jnp.float32),
            pltpu.VMEM(square, bf16),
            pltpu.VMEM(square, bf16),
            pltpu.VMEM((128, tile_rows, tile_cols), bf16),
            pltpu.SemaphoreType.DMA((7,)),
            pltpu.SemaphoreType.DMA((5,)),
            pltpu.SemaphoreType.DMA,
            pltpu.SemaphoreType.DMA,
            pltpu.SemaphoreType.DMA,
            pltpu.SemaphoreType.DMA,
        ],
        compiler_params=pltpu.CompilerParams(
            collective_id=0, has_side_effects=True, vmem_limit_bytes=56 << 20
        ),
    )(
        inverse,
        block_slot,
        codes,
        scales,
        left_basis[0],
        right_basis[0],
        first_moment[0],
        second_moment[0],
        left_gram[0],
        right_gram[0],
    )
    update = outs[0].reshape(block_rows, block_cols, tile_rows, tile_cols)
    return (update.transpose(0, 2, 1, 3),) + tuple(a[None] for a in outs[1:])


def solution(mesh):
    whole = P(("dp", "tensor"), None, None)
    tiles = P(None, "tensor", None, "dp")
    return jax.shard_map(
        on_device,
        mesh=mesh,
        in_specs=(tiles, tiles, P()) + (whole,) * 6,
        out_specs=(tiles,) + (whole,) * 4,
        check_vma=False,
    )
```

```python
import functools

import jax
import jax.numpy as jnp
from jax import lax
from jax.experimental import pallas as pl
from jax.experimental.pallas import tpu as pltpu
from jax.sharding import PartitionSpec as P

beta_first = 0.9
beta_second = 0.95
gram_decay = 0.9
epsilon = 1e-08

CHUNK = 256
SLICE = 16
PART = 128


def nt(a, b):
    return lax.dot_general(a, b, (((1,), (1,)), ((), ())), preferred_element_type=jnp.float32)


def nn(a, b):
    return jnp.dot(a, b, preferred_element_type=jnp.float32)


def digits(i, *sizes):
    out = []
    for n in sizes:
        out.append(lax.rem(i, n))
        i = i // n
    return out


def kernel(
    slots_hbm,
    codes_hbm,
    scales_hbm,
    left_hbm,
    right_hbm,
    first_hbm,
    second_hbm,
    lgram_hbm,
    rgram_hbm,
    arrived,
    first_new,
    second_new,
    lgram_new,
    rgram_new,
    slots,
    scales,
    table,
    inverse,
    codes,
    stage,
    grad,
    flip,
    left,
    left_t,
    right,
    first,
    second,
    lgram,
    rgram,
    half,
    direction,
    back,
    rotated,
    turned_even,
    turned_odd,
    half_back,
    load_sem,
    table_sem,
    grad_send,
    grad_recv,
    back_send,
    back_recv,
):
    blocks, tile_rows, tile_cols = codes.shape
    side = grad.shape[0]
    dp_index = lax.axis_index("dp")
    t_index = lax.axis_index("tensor")
    z = dp_index // 2
    x, y = t_index // 4, lax.rem(t_index, 4)
    me = dp_index * 16 + t_index
    owner = me < blocks

    loads = [
        pltpu.make_async_copy(src, dst, load_sem.at[n])
        for n, (src, dst) in enumerate(
            (
                (slots_hbm, slots),
                (scales_hbm, scales),
                (codes_hbm, codes),
                (left_hbm, left),
                (right_hbm, right),
                (first_hbm, first),
                (second_hbm, second),
                (lgram_hbm, lgram),
                (rgram_hbm, rgram),
            )
        )
    ]
    for copy in loads[:3]:
        copy.start()

    barrier = pltpu.get_barrier_semaphore()

    def greet(i):
        o = lax.rem(me + i, 128)
        pl.semaphore_signal(
            barrier, inc=1, device_id={"dp": o // 16, "tensor": lax.rem(o, 16)}
        )

    @pl.loop(1, 72)
    def _(i):
        greet(i)

    loads[0].wait()
    down = lax.broadcasted_iota(jnp.int32, (blocks, blocks), 0)
    across = lax.broadcasted_iota(jnp.int32, (blocks, blocks), 1)
    column = jnp.sum(jnp.where(down == across, slots[...], 0), axis=1, keepdims=True)
    table[...] = jnp.max(jnp.where(column == across, down, 0), axis=0, keepdims=True)
    fetch = pltpu.make_async_copy(table, inverse, table_sem)
    fetch.start()

    loads[1].wait()
    eye = (
        lax.broadcasted_iota(jnp.int32, (tile_rows, tile_rows), 0)
        == lax.broadcasted_iota(jnp.int32, (tile_rows, tile_rows), 1)
    ).astype(jnp.bfloat16)
    scale_t = nt(eye, scales[...])
    lane = lax.broadcasted_iota(jnp.int32, (tile_rows, blocks), 1)
    lane_block = lax.rem(lane, 8) * 14 + lane // 8

    def tile_at(ref, o):
        rows = pl.multiple_of(lax.rem(o, 16) * tile_rows, tile_rows)
        cols = pl.multiple_of((o // 16) * tile_cols, tile_cols)
        return ref.at[pl.ds(rows, tile_rows), pl.ds(cols, tile_cols)]

    fetch.wait()
    loads[2].wait()
    for copy in loads[3:]:
        copy.start()

    @pl.loop(0, blocks // 4)
    def _(i):
        greet(72 + 2 * i)
        greet(73 + 2 * i)
        for q in range(4):
            o = 4 * i + q
            block = inverse[0, o]
            scale = jnp.sum(
                jnp.where(lane_block == block, scale_t, 0.0), axis=1, keepdims=True
            )
            stage[o] = (codes[block].astype(jnp.float32) * scale).astype(jnp.bfloat16)

    pl.semaphore_wait(barrier, 127)

    @pl.loop(0, 128)
    def _(i):
        dzb, a, b, zp, core = digits(i, 2, 4, 4, 2, 2)
        z2 = lax.rem(z + 2 * dzb + 1 - zp, 4)
        x2 = lax.rem(x + a, 4)
        y2 = lax.rem(y + a + b, 4)
        o = (z2 * 2 + core) * 16 + x2 * 4 + y2

        @pl.when(jnp.logical_and(o < blocks, o != me))
        def _():
            pltpu.make_async_remote_copy(
                stage.at[o],
                tile_at(grad, me),
                grad_send,
                grad_recv.at[zp],
                device_id={"dp": z2 * 2 + core, "tensor": x2 * 4 + y2},
            ).start()

    @pl.when(owner)
    def _():
        pltpu.sync_copy(stage.at[me], tile_at(grad, me))

    @pl.when(jnp.logical_not(owner))
    def _():
        grad[...] = jnp.zeros_like(grad)

    def chunked(body):
        @pl.loop(0, side // CHUNK)
        def _(i):
            body(pl.ds(pl.multiple_of(i * CHUNK, CHUNK), CHUNK))

    loads[3].wait()

    def flip_left(rows):
        left_t[rows, :] = left[:, rows].T

    chunked(flip_left)
    for copy in loads[4:]:
        copy.wait()

    def span(k):
        return pl.ds(pl.multiple_of(lax.rem(z + k, 4) * CHUNK, CHUNK), CHUNK)

    def to_half(k):
        half[:, span(k)] = nn(left_t[...], grad[:, span(k)]).astype(jnp.bfloat16)

    def turn(rows, k):
        return nn(half[rows, span(k)], right[span(k), :])

    @pl.when(owner)
    def _():
        wait_tiles(arrived, 64, grad_recv.at[0])

    to_half(1)
    to_half(3)

    def turn_first(rows):
        rotated[rows, :] = turn(rows, 1) + turn(rows, 3)

    chunked(turn_first)

    @pl.when(owner)
    def _():
        wait_tiles(arrived, 63, grad_recv.at[1])

    to_half(2)
    to_half(0)

    def step(rows, turned):
        m = beta_first * first[rows, :].astype(jnp.float32) + (1.0 - beta_first) * turned
        v = (
            beta_second * second[rows, :].astype(jnp.float32)
            + (1.0 - beta_second) * turned * turned
        )
        root = v * lax.rsqrt(v)
        direction[rows, :] = (m / (root + epsilon)).astype(jnp.bfloat16)
        first_new[rows, :] = m.astype(jnp.bfloat16)
        second_new[rows, :] = v.astype(jnp.bfloat16)

    parts = side // PART
    for i in range(parts + 1):
        if i < parts:
            rows = pl.ds(i * PART, PART)
            turned = turned_odd if i % 2 else turned_even
            turned[...] = rotated[rows, :] + turn(rows, 2) + turn(rows, 0)
        if i > 0:
            turned = turned_even if i % 2 else turned_odd
            for j in range(PART // SLICE):
                step(
                    pl.ds((i - 1) * PART + j * SLICE, SLICE),
                    turned[pl.ds(j * SLICE, SLICE), :],
                )

    for parity in (1, 0):

        @pl.loop(0, 2)
        def _(k):
            x2 = lax.rem(x + 2 * k + parity, 4)
            rows = pl.ds(pl.multiple_of(x2 * CHUNK, CHUNK), CHUNK)
            half_back[...] = nn(left[rows, :], direction[...]).astype(jnp.bfloat16)
            back[rows, :] = nt(half_back[...], right[...]).astype(jnp.bfloat16)

        @pl.when(owner)
        def _():
            @pl.loop(0, 64)
            def _(i):
                dzb, k, dyb, core, zp, yp = digits(i, 2, 2, 2, 2, 2, 2)
                z2 = lax.rem(z + 2 * dzb + 1 - zp, 4)
                x2 = lax.rem(x + 2 * k + parity, 4)
                y2 = lax.rem(y + 2 * dyb + yp, 4)
                o = (z2 * 2 + core) * 16 + x2 * 4 + y2

                @pl.when(o != me)
                def _():
                    pltpu.make_async_remote_copy(
                        tile_at(back, o),
                        arrived.at[me],
                        back_send,
                        back_recv,
                        device_id={"dp": z2 * 2 + core, "tensor": x2 * 4 + y2},
                    ).start()

    @pl.when(owner)
    def _():
        pltpu.sync_copy(tile_at(back, me), arrived.at[me])

    def flip_grad(rows):
        flip[rows, :] = grad[:, rows].T

    chunked(flip_grad)

    def grams(rows):
        lgram_new[rows, :] = (
            gram_decay * lgram[rows, :].astype(jnp.float32)
            + (1.0 - gram_decay) * nt(grad[rows, :], grad[...])
        ).astype(jnp.bfloat16)
        rgram_new[rows, :] = (
            gram_decay * rgram[rows, :].astype(jnp.float32)
            + (1.0 - gram_decay) * nt(flip[rows, :], flip[...])
        ).astype(jnp.bfloat16)

    chunked(grams)

    @pl.when(owner)
    def _():
        wait_tiles(arrived, 111, grad_send)
        wait_tiles(arrived, 127, back_send)
        wait_tiles(arrived, 111, back_recv)

    @pl.when(jnp.logical_not(owner))
    def _():
        wait_tiles(arrived, 112, grad_send)
        wait_tiles(arrived, 112, back_recv)


def wait_tiles(ref, tiles, sem):
    part = ref.at[pl.ds(0, tiles)]
    pltpu.make_async_copy(part, part, sem).wait()


def publish(slots, arrived, *refs):
    kept, update, made, tile_sem, sems = refs[:4], refs[4], refs[5:9], refs[9], refs[10]
    copies = [
        pltpu.make_async_copy(a, b, sems.at[n]) for n, (a, b) in enumerate(zip(kept, made))
    ]
    for copy in copies:
        copy.start()

    @pl.loop(0, update.shape[0])
    def _(b):
        pltpu.make_async_copy(arrived.at[slots[b]], update.at[b], tile_sem).start()

    every = arrived.at[pl.ds(0, update.shape[0])]
    pltpu.make_async_copy(every, update, tile_sem).wait()
    for copy in copies:
        copy.wait()


def on_device(
    grad_codes,
    grad_scales,
    block_slot,
    left_basis,
    right_basis,
    first_moment,
    second_moment,
    left_gram,
    right_gram,
):
    block_rows, tile_rows, block_cols, tile_cols = grad_codes.shape
    blocks = block_rows * block_cols
    side = left_basis.shape[1]
    bf16 = jnp.bfloat16
    codes = grad_codes.transpose(0, 2, 1, 3).reshape(blocks, tile_rows, tile_cols)
    scales = grad_scales.transpose(2, 3, 0, 1).reshape(blocks, tile_rows)
    held = [
        pltpu.with_memory_space_constraint(a, pltpu.HBM)
        for a in (
            block_slot.reshape(1, blocks),
            codes,
            scales,
            left_basis[0],
            right_basis[0],
            first_moment[0],
            second_moment[0],
            left_gram[0],
            right_gram[0],
        )
    ]
    square = (side, side)
    anywhere = pl.BlockSpec(memory_space=pltpu.HBM)
    outs = pl.pallas_call(
        kernel,
        name="soap_exchange",
        out_shape=[pltpu.VMEM((128, tile_rows, tile_cols), bf16)]
        + [pltpu.VMEM(square, bf16)] * 4,
        in_specs=[anywhere] * 9,
        out_specs=[pl.BlockSpec(memory_space=pltpu.VMEM)] * 5,
        scratch_shapes=[
            pltpu.VMEM((1, blocks), jnp.int32),
            pltpu.VMEM((blocks, tile_rows), bf16),
            pltpu.VMEM((1, blocks), jnp.int32),
            pltpu.SMEM((1, blocks), jnp.int32),
            pltpu.VMEM((blocks, tile_rows, tile_cols), bf16),
            pltpu.VMEM((blocks, tile_rows, tile_cols), bf16),
        ]
        + [pltpu.VMEM(square, bf16)] * 12
        + [
            pltpu.VMEM(square, jnp.float32),
            pltpu.VMEM((PART, side), jnp.float32),
            pltpu.VMEM((PART, side), jnp.float32),
            pltpu.VMEM((CHUNK, side), bf16),
            pltpu.SemaphoreType.DMA((9,)),
            pltpu.SemaphoreType.DMA,
            pltpu.SemaphoreType.DMA,
            pltpu.SemaphoreType.DMA((2,)),
            pltpu.SemaphoreType.DMA,
            pltpu.SemaphoreType.DMA,
        ],
        compiler_params=pltpu.CompilerParams(
            collective_id=0, has_side_effects=True, vmem_limit_bytes=40 << 20
        ),
    )(*held)
    outs = pl.pallas_call(
        publish,
        name="publish",
        out_shape=[jax.ShapeDtypeStruct(codes.shape, bf16)]
        + [jax.ShapeDtypeStruct(square, bf16)] * 4,
        in_specs=[pl.BlockSpec(memory_space=pltpu.SMEM)]
        + [pl.BlockSpec(memory_space=pltpu.VMEM)] * 5,
        out_specs=[pl.BlockSpec(memory_space=pltpu.HBM)] * 5,
        scratch_shapes=[pltpu.SemaphoreType.DMA, pltpu.SemaphoreType.DMA((4,))],
        compiler_params=pltpu.CompilerParams(vmem_limit_bytes=1 << 20),
    )(block_slot, *[pltpu.with_memory_space_constraint(a, pltpu.VMEM) for a in outs])
    update = outs[0].reshape(block_rows, block_cols, tile_rows, tile_cols)
    return (update.transpose(0, 2, 1, 3),) + tuple(a[None] for a in outs[1:])


def solution(mesh):
    whole = P(("dp", "tensor"), None, None)
    tiles = P(None, "tensor", None, "dp")
    return jax.shard_map(
        on_device,
        mesh=mesh,
        in_specs=(tiles, tiles, P()) + (whole,) * 6,
        out_specs=(tiles,) + (whole,) * 4,
        check_vma=False,
    )
```

```python
import functools

import jax
import jax.numpy as jnp
from jax import lax
from jax.experimental import pallas as pl
from jax.experimental.pallas import tpu as pltpu
from jax.sharding import PartitionSpec as P

beta_first = 0.9
beta_second = 0.95
gram_decay = 0.9
epsilon = 1e-08

CHUNK = 256
SLICE = 16
PART = 128


def nt(a, b):
    return lax.dot_general(a, b, (((1,), (1,)), ((), ())), preferred_element_type=jnp.float32)


def nn(a, b):
    return jnp.dot(a, b, preferred_element_type=jnp.float32)


def digits(i, *sizes):
    out = []
    for n in sizes:
        out.append(lax.rem(i, n))
        i = i // n
    return out


def kernel(
    slots_hbm,
    codes_hbm,
    scales_hbm,
    left_hbm,
    right_hbm,
    first_hbm,
    second_hbm,
    lgram_hbm,
    rgram_hbm,
    arrived,
    first_new,
    second_new,
    lgram_new,
    rgram_new,
    slots,
    scales,
    table,
    inverse,
    codes,
    stage,
    grad,
    flip,
    left,
    left_t,
    right,
    first,
    second,
    lgram,
    rgram,
    half,
    direction,
    back,
    rotated,
    turned_even,
    turned_odd,
    half_back,
    load_sem,
    table_sem,
    grad_send,
    grad_recv,
    back_send,
    back_recv,
):
    blocks, tile_rows, tile_cols = codes.shape
    side = grad.shape[0]
    dp_index = lax.axis_index("dp")
    t_index = lax.axis_index("tensor")
    z, c = dp_index // 2, lax.rem(dp_index, 2)
    x, y = t_index // 4, lax.rem(t_index, 4)
    me = dp_index * 16 + t_index
    owner = me < blocks

    loads = [
        pltpu.make_async_copy(src, dst, load_sem.at[n])
        for n, (src, dst) in enumerate(
            (
                (slots_hbm, slots),
                (scales_hbm, scales),
                (codes_hbm, codes),
                (left_hbm, left),
                (right_hbm, right),
                (first_hbm, first),
                (second_hbm, second),
                (lgram_hbm, lgram),
                (rgram_hbm, rgram),
            )
        )
    ]
    for copy in loads[:3]:
        copy.start()

    barrier = pltpu.get_barrier_semaphore()

    def greet(i):
        o = lax.rem(me + i, 128)
        pl.semaphore_signal(
            barrier, inc=1, device_id={"dp": o // 16, "tensor": lax.rem(o, 16)}
        )

    @pl.loop(1, 128)
    def _(i):
        greet(i)

    loads[0].wait()
    down = lax.broadcasted_iota(jnp.int32, (blocks, blocks), 0)
    across = lax.broadcasted_iota(jnp.int32, (blocks, blocks), 1)
    column = jnp.sum(jnp.where(down == across, slots[...], 0), axis=1, keepdims=True)
    table[...] = jnp.max(jnp.where(column == across, down, 0), axis=0, keepdims=True)
    fetch = pltpu.make_async_copy(table, inverse, table_sem)
    fetch.start()

    loads[1].wait()
    eye = (
        lax.broadcasted_iota(jnp.int32, (tile_rows, tile_rows), 0)
        == lax.broadcasted_iota(jnp.int32, (tile_rows, tile_rows), 1)
    ).astype(jnp.bfloat16)
    scale_t = nt(eye, scales[...])
    lane = lax.broadcasted_iota(jnp.int32, (tile_rows, blocks), 1)
    lane_block = lax.rem(lane, 8) * 14 + lane // 8

    def tile_at(ref, o):
        rows = pl.multiple_of(lax.rem(o, 16) * tile_rows, tile_rows)
        cols = pl.multiple_of((o // 16) * tile_cols, tile_cols)
        return ref.at[pl.ds(rows, tile_rows), pl.ds(cols, tile_cols)]

    fetch.wait()
    loads[2].wait()
    for copy in loads[3:]:
        copy.start()

    @pl.loop(0, blocks // 4)
    def _(i):
        for q in range(4):
            o = 4 * i + q
            block = inverse[0, o]
            scale = jnp.sum(
                jnp.where(lane_block == block, scale_t, 0.0), axis=1, keepdims=True
            )
            stage[o] = (codes[block].astype(jnp.float32) * scale).astype(jnp.bfloat16)

    pl.semaphore_wait(barrier, 127)

    @pl.loop(0, 128)
    def _(i):
        dzb, a, b, zp, core = digits(i, 2, 4, 4, 2, 2)
        z2 = lax.rem(z + 2 * dzb + 1 - zp, 4)
        x2 = lax.rem(x + a, 4)
        y2 = lax.rem(y + a + b, 4)
        o = (z2 * 2 + core) * 16 + x2 * 4 + y2

        @pl.when(jnp.logical_and(o < blocks, o != me))
        def _():
            pltpu.make_async_remote_copy(
                stage.at[o],
                tile_at(grad, me),
                grad_send,
                grad_recv.at[zp],
                device_id={"dp": z2 * 2 + core, "tensor": x2 * 4 + y2},
            ).start()

    @pl.when(owner)
    def _():
        pltpu.sync_copy(stage.at[me], tile_at(grad, me))

    @pl.when(jnp.logical_not(owner))
    def _():
        grad[...] = jnp.zeros_like(grad)

    def chunked(body):
        @pl.loop(0, side // CHUNK)
        def _(i):
            body(pl.ds(pl.multiple_of(i * CHUNK, CHUNK), CHUNK))

    loads[3].wait()

    def flip_left(rows):
        left_t[rows, :] = left[:, rows].T

    chunked(flip_left)
    for copy in loads[4:]:
        copy.wait()

    def span(k):
        return pl.ds(pl.multiple_of(lax.rem(z + k, 4) * CHUNK, CHUNK), CHUNK)

    def to_half(k):
        half[:, span(k)] = nn(left_t[...], grad[:, span(k)]).astype(jnp.bfloat16)

    def turn(rows, k):
        return nn(half[rows, span(k)], right[span(k), :])

    @pl.when(owner)
    def _():
        wait_tiles(arrived, 64, grad_recv.at[0])

    to_half(1)
    to_half(3)

    def turn_first(rows):
        rotated[rows, :] = turn(rows, 1) + turn(rows, 3)

    chunked(turn_first)

    @pl.when(owner)
    def _():
        wait_tiles(arrived, 63, grad_recv.at[1])

    to_half(2)
    to_half(0)

    def step(rows, turned):
        m = beta_first * first[rows, :].astype(jnp.float32) + (1.0 - beta_first) * turned
        v = (
            beta_second * second[rows, :].astype(jnp.float32)
            + (1.0 - beta_second) * turned * turned
        )
        root = v * lax.rsqrt(v) + epsilon
        direction[rows, :] = (m * lax.rsqrt(root * root)).astype(jnp.bfloat16)
        first_new[rows, :] = m.astype(jnp.bfloat16)
        second_new[rows, :] = v.astype(jnp.bfloat16)

    parts = side // PART
    for i in range(parts + 1):
        if i < parts:
            rows = pl.ds(i * PART, PART)
            turned = turned_odd if i % 2 else turned_even
            turned[...] = rotated[rows, :] + turn(rows, 2) + turn(rows, 0)
        if i > 0:
            turned = turned_even if i % 2 else turned_odd
            for j in range(PART // SLICE):
                step(
                    pl.ds((i - 1) * PART + j * SLICE, SLICE),
                    turned[pl.ds(j * SLICE, SLICE), :],
                )

    @pl.loop(0, 4)
    def _(turn_at):
        yp, even = lax.rem(turn_at, 2), turn_at // 2
        places = [
            pl.multiple_of(
                lax.rem(x + 2 * k + 1 - even, 4) * CHUNK
                + lax.rem(y + 2 * dyb + yp, 4) * tile_rows,
                tile_rows,
            )
            for k in range(2)
            for dyb in range(2)
        ]
        picked = [left[pl.ds(p, tile_rows), :] for p in places]
        half_back[...] = nn(jnp.concatenate(picked, axis=0), direction[...]).astype(
            jnp.bfloat16
        )
        out = nt(half_back[...], right[...]).astype(jnp.bfloat16)
        for n, p in enumerate(places):
            back[pl.ds(p, tile_rows), :] = out[n * tile_rows : (n + 1) * tile_rows]

        @pl.when(owner)
        def _():
            @pl.loop(0, 32)
            def _(i):
                core, dzb, k, dyb, zp = digits(i, 2, 2, 2, 2, 2)
                core = lax.rem(core + c, 2)
                z2 = lax.rem(z + 2 * (dzb + c) + 1 - zp, 4)
                x2 = lax.rem(x + 2 * k + 1 - even, 4)
                y2 = lax.rem(y + 2 * dyb + yp, 4)
                o = (z2 * 2 + core) * 16 + x2 * 4 + y2

                @pl.when(o != me)
                def _():
                    pltpu.make_async_remote_copy(
                        tile_at(back, o),
                        arrived.at[me],
                        back_send,
                        back_recv,
                        device_id={"dp": z2 * 2 + core, "tensor": x2 * 4 + y2},
                    ).start()

    @pl.when(owner)
    def _():
        pltpu.sync_copy(tile_at(back, me), arrived.at[me])

    def flip_grad(rows):
        flip[rows, :] = grad[:, rows].T

    chunked(flip_grad)

    def grams(rows):
        lgram_new[rows, :] = (
            gram_decay * lgram[rows, :].astype(jnp.float32)
            + (1.0 - gram_decay) * nt(grad[rows, :], grad[...])
        ).astype(jnp.bfloat16)
        rgram_new[rows, :] = (
            gram_decay * rgram[rows, :].astype(jnp.float32)
            + (1.0 - gram_decay) * nt(flip[rows, :], flip[...])
        ).astype(jnp.bfloat16)

    chunked(grams)

    @pl.when(owner)
    def _():
        wait_tiles(arrived, 111, grad_send)
        wait_tiles(arrived, 127, back_send)
        wait_tiles(arrived, 111, back_recv)

    @pl.when(jnp.logical_not(owner))
    def _():
        wait_tiles(arrived, 112, grad_send)
        wait_tiles(arrived, 112, back_recv)


def wait_tiles(ref, tiles, sem):
    part = ref.at[pl.ds(0, tiles)]
    pltpu.make_async_copy(part, part, sem).wait()


def publish(slots, arrived, *refs):
    kept, update, made, tile_sem, sems = refs[:4], refs[4], refs[5:9], refs[9], refs[10]
    copies = [
        pltpu.make_async_copy(a, b, sems.at[n]) for n, (a, b) in enumerate(zip(kept, made))
    ]
    for copy in copies:
        copy.start()

    @pl.loop(0, update.shape[0])
    def _(b):
        pltpu.make_async_copy(arrived.at[slots[b]], update.at[b], tile_sem).start()

    every = arrived.at[pl.ds(0, update.shape[0])]
    pltpu.make_async_copy(every, update, tile_sem).wait()
    for copy in copies:
        copy.wait()


def on_device(
    grad_codes,
    grad_scales,
    block_slot,
    left_basis,
    right_basis,
    first_moment,
    second_moment,
    left_gram,
    right_gram,
):
    block_rows, tile_rows, block_cols, tile_cols = grad_codes.shape
    blocks = block_rows * block_cols
    side = left_basis.shape[1]
    bf16 = jnp.bfloat16
    codes = grad_codes.transpose(0, 2, 1, 3).reshape(blocks, tile_rows, tile_cols)
    scales = grad_scales.transpose(2, 3, 0, 1).reshape(blocks, tile_rows)
    held = [
        pltpu.with_memory_space_constraint(a, pltpu.HBM)
        for a in (
            block_slot.reshape(1, blocks),
            codes,
            scales,
            left_basis[0],
            right_basis[0],
            first_moment[0],
            second_moment[0],
            left_gram[0],
            right_gram[0],
        )
    ]
    square = (side, side)
    anywhere = pl.BlockSpec(memory_space=pltpu.HBM)
    outs = pl.pallas_call(
        kernel,
        name="soap_exchange",
        out_shape=[pltpu.VMEM((128, tile_rows, tile_cols), bf16)]
        + [pltpu.VMEM(square, bf16)] * 4,
        in_specs=[anywhere] * 9,
        out_specs=[pl.BlockSpec(memory_space=pltpu.VMEM)] * 5,
        scratch_shapes=[
            pltpu.VMEM((1, blocks), jnp.int32),
            pltpu.VMEM((blocks, tile_rows), bf16),
            pltpu.VMEM((1, blocks), jnp.int32),
            pltpu.SMEM((1, blocks), jnp.int32),
            pltpu.VMEM((blocks, tile_rows, tile_cols), bf16),
            pltpu.VMEM((blocks, tile_rows, tile_cols), bf16),
        ]
        + [pltpu.VMEM(square, bf16)] * 12
        + [
            pltpu.VMEM(square, jnp.float32),
            pltpu.VMEM((PART, side), jnp.float32),
            pltpu.VMEM((PART, side), jnp.float32),
            pltpu.VMEM((CHUNK, side), bf16),
            pltpu.SemaphoreType.DMA((9,)),
            pltpu.SemaphoreType.DMA,
            pltpu.SemaphoreType.DMA,
            pltpu.SemaphoreType.DMA((2,)),
            pltpu.SemaphoreType.DMA,
            pltpu.SemaphoreType.DMA,
        ],
        compiler_params=pltpu.CompilerParams(
            collective_id=0, has_side_effects=True, vmem_limit_bytes=40 << 20
        ),
    )(*held)
    outs = pl.pallas_call(
        publish,
        name="publish",
        out_shape=[jax.ShapeDtypeStruct(codes.shape, bf16)]
        + [jax.ShapeDtypeStruct(square, bf16)] * 4,
        in_specs=[pl.BlockSpec(memory_space=pltpu.SMEM)]
        + [pl.BlockSpec(memory_space=pltpu.VMEM)] * 5,
        out_specs=[pl.BlockSpec(memory_space=pltpu.HBM)] * 5,
        scratch_shapes=[pltpu.SemaphoreType.DMA, pltpu.SemaphoreType.DMA((4,))],
        compiler_params=pltpu.CompilerParams(vmem_limit_bytes=1 << 20),
    )(block_slot, *[pltpu.with_memory_space_constraint(a, pltpu.VMEM) for a in outs])
    update = outs[0].reshape(block_rows, block_cols, tile_rows, tile_cols)
    return (update.transpose(0, 2, 1, 3),) + tuple(a[None] for a in outs[1:])


def solution(mesh):
    whole = P(("dp", "tensor"), None, None)
    tiles = P(None, "tensor", None, "dp")
    return jax.shard_map(
        on_device,
        mesh=mesh,
        in_specs=(tiles, tiles, P()) + (whole,) * 6,
        out_specs=(tiles,) + (whole,) * 4,
        check_vma=False,
    )
```

```python
import functools

import jax
import jax.numpy as jnp
from jax import lax
from jax.experimental import pallas as pl
from jax.experimental.pallas import tpu as pltpu
from jax.sharding import PartitionSpec as P

beta_first = 0.9
beta_second = 0.95
gram_decay = 0.9
epsilon = 1e-08

CHUNK = 256
SLICE = 16
PART = 128


def nt(a, b):
    return lax.dot_general(a, b, (((1,), (1,)), ((), ())), preferred_element_type=jnp.float32)


def nn(a, b):
    return jnp.dot(a, b, preferred_element_type=jnp.float32)


def digits(i, *sizes):
    out = []
    for n in sizes:
        out.append(lax.rem(i, n))
        i = i // n
    return out


def kernel(
    slots_hbm,
    codes_hbm,
    scales_hbm,
    left_hbm,
    right_hbm,
    first_hbm,
    second_hbm,
    lgram_hbm,
    rgram_hbm,
    arrived,
    first_new,
    second_new,
    lgram_new,
    rgram_new,
    slots,
    scales,
    table,
    inverse,
    codes,
    stage,
    grad,
    flip,
    left,
    left_t,
    right,
    first,
    second,
    lgram,
    rgram,
    half,
    direction,
    back,
    rotated,
    turned_even,
    turned_odd,
    half_back,
    load_sem,
    table_sem,
    grad_send,
    grad_recv,
    back_send,
    back_recv,
):
    blocks, tile_rows, tile_cols = codes.shape
    side = grad.shape[0]
    dp_index = lax.axis_index("dp")
    t_index = lax.axis_index("tensor")
    z, c = dp_index // 2, lax.rem(dp_index, 2)
    x, y = t_index // 4, lax.rem(t_index, 4)
    me = dp_index * 16 + t_index
    owner = me < blocks

    loads = [
        pltpu.make_async_copy(src, dst, load_sem.at[n])
        for n, (src, dst) in enumerate(
            (
                (slots_hbm, slots),
                (scales_hbm, scales),
                (codes_hbm, codes),
                (left_hbm, left),
                (right_hbm, right),
                (first_hbm, first),
                (second_hbm, second),
                (lgram_hbm, lgram),
                (rgram_hbm, rgram),
            )
        )
    ]
    for copy in loads[:3]:
        copy.start()

    barrier = pltpu.get_barrier_semaphore()

    def greet(i):
        o = lax.rem(me + i, 128)
        pl.semaphore_signal(
            barrier, inc=1, device_id={"dp": o // 16, "tensor": lax.rem(o, 16)}
        )

    @pl.loop(0, 18)
    def _(i):
        for q in range(7):
            greet(1 + 7 * i + q)

    greet(127)

    loads[0].wait()
    down = lax.broadcasted_iota(jnp.int32, (blocks, blocks), 0)
    across = lax.broadcasted_iota(jnp.int32, (blocks, blocks), 1)
    column = jnp.sum(jnp.where(down == across, slots[...], 0), axis=1, keepdims=True)
    table[...] = jnp.max(jnp.where(column == across, down, 0), axis=0, keepdims=True)
    fetch = pltpu.make_async_copy(table, inverse, table_sem)
    fetch.start()

    loads[1].wait()
    eye = (
        lax.broadcasted_iota(jnp.int32, (tile_rows, tile_rows), 0)
        == lax.broadcasted_iota(jnp.int32, (tile_rows, tile_rows), 1)
    ).astype(jnp.bfloat16)
    scale_t = nt(eye, scales[...])
    lane = lax.broadcasted_iota(jnp.int32, (tile_rows, blocks), 1)
    lane_block = lax.rem(lane, 8) * 14 + lane // 8

    def tile_at(ref, o):
        rows = pl.multiple_of(lax.rem(o, 16) * tile_rows, tile_rows)
        cols = pl.multiple_of((o // 16) * tile_cols, tile_cols)
        return ref.at[pl.ds(rows, tile_rows), pl.ds(cols, tile_cols)]

    fetch.wait()
    loads[2].wait()
    for copy in loads[3:]:
        copy.start()

    @pl.loop(0, blocks // 4)
    def _(i):
        for q in range(4):
            o = 4 * i + q
            block = inverse[0, o]
            scale = jnp.sum(
                jnp.where(lane_block == block, scale_t, 0.0), axis=1, keepdims=True
            )
            stage[o] = (codes[block].astype(jnp.float32) * scale).astype(jnp.bfloat16)

    pl.semaphore_wait(barrier, 127)

    @pl.loop(0, 128)
    def _(i):
        dzb, a, b, zp, core = digits(i, 2, 4, 4, 2, 2)
        z2 = lax.rem(z + 2 * dzb + 1 - zp, 4)
        x2 = lax.rem(x + a, 4)
        y2 = lax.rem(y + a + b, 4)
        o = (z2 * 2 + core) * 16 + x2 * 4 + y2

        @pl.when(jnp.logical_and(o < blocks, o != me))
        def _():
            pltpu.make_async_remote_copy(
                stage.at[o],
                tile_at(grad, me),
                grad_send,
                grad_recv.at[zp],
                device_id={"dp": z2 * 2 + core, "tensor": x2 * 4 + y2},
            ).start()

    @pl.when(owner)
    def _():
        pltpu.sync_copy(stage.at[me], tile_at(grad, me))

    @pl.when(jnp.logical_not(owner))
    def _():
        grad[...] = jnp.zeros_like(grad)

    def chunked(body):
        @pl.loop(0, side // CHUNK)
        def _(i):
            body(pl.ds(pl.multiple_of(i * CHUNK, CHUNK), CHUNK))

    loads[3].wait()

    def flip_left(rows):
        left_t[rows, :] = left[:, rows].T

    chunked(flip_left)
    for copy in loads[4:]:
        copy.wait()

    def span(k):
        return pl.ds(pl.multiple_of(lax.rem(z + k, 4) * CHUNK, CHUNK), CHUNK)

    def to_half(k):
        half[:, span(k)] = nn(left_t[...], grad[:, span(k)]).astype(jnp.bfloat16)

    def turn(rows, k):
        return nn(half[rows, span(k)], right[span(k), :])

    @pl.when(owner)
    def _():
        wait_tiles(arrived, 64, grad_recv.at[0])

    to_half(1)
    to_half(3)

    def turn_first(rows):
        rotated[rows, :] = turn(rows, 1) + turn(rows, 3)

    chunked(turn_first)

    @pl.when(owner)
    def _():
        wait_tiles(arrived, 63, grad_recv.at[1])

    to_half(2)
    to_half(0)

    def step(rows, turned):
        m = beta_first * first[rows, :].astype(jnp.float32) + (1.0 - beta_first) * turned
        v = (
            beta_second * second[rows, :].astype(jnp.float32)
            + (1.0 - beta_second) * turned * turned
        )
        root = v * lax.rsqrt(v) + epsilon
        direction[rows, :] = (m * lax.rsqrt(root * root)).astype(jnp.bfloat16)

    def keep(rows):
        turned = rotated[rows, :]
        m = beta_first * first[rows, :].astype(jnp.float32) + (1.0 - beta_first) * turned
        v = (
            beta_second * second[rows, :].astype(jnp.float32)
            + (1.0 - beta_second) * turned * turned
        )
        first_new[rows, :] = m.astype(jnp.bfloat16)
        second_new[rows, :] = v.astype(jnp.bfloat16)

    parts = side // PART
    for i in range(parts + 1):
        if i < parts:
            rows = pl.ds(i * PART, PART)
            rotated[rows, :] = rotated[rows, :] + turn(rows, 2) + turn(rows, 0)
        if i > 0:
            for j in range(PART // SLICE):
                step(
                    pl.ds((i - 1) * PART + j * SLICE, SLICE),
                    rotated[pl.ds((i - 1) * PART + j * SLICE, SLICE), :],
                )

    @pl.loop(0, 4)
    def _(turn_at):
        yp, even = lax.rem(turn_at, 2), turn_at // 2
        places = [
            pl.multiple_of(
                lax.rem(x + 2 * k + 1 - even, 4) * CHUNK
                + lax.rem(y + 2 * dyb + yp, 4) * tile_rows,
                tile_rows,
            )
            for k in range(2)
            for dyb in range(2)
        ]
        picked = [left[pl.ds(p, tile_rows), :] for p in places]
        half_back[...] = nn(jnp.concatenate(picked, axis=0), direction[...]).astype(
            jnp.bfloat16
        )
        out = nt(half_back[...], right[...]).astype(jnp.bfloat16)
        for n, p in enumerate(places):
            back[pl.ds(p, tile_rows), :] = out[n * tile_rows : (n + 1) * tile_rows]

        @pl.when(owner)
        def _():
            @pl.loop(0, 32)
            def _(i):
                core, dzb, k, dyb, zp = digits(i, 2, 2, 2, 2, 2)
                core = lax.rem(core + c, 2)
                z2 = lax.rem(z + 2 * (dzb + c) + 1 - zp, 4)
                x2 = lax.rem(x + 2 * k + 1 - even, 4)
                y2 = lax.rem(y + 2 * dyb + yp, 4)
                o = (z2 * 2 + core) * 16 + x2 * 4 + y2

                @pl.when(o != me)
                def _():
                    pltpu.make_async_remote_copy(
                        tile_at(back, o),
                        arrived.at[me],
                        back_send,
                        back_recv,
                        device_id={"dp": z2 * 2 + core, "tensor": x2 * 4 + y2},
                    ).start()

    @pl.when(owner)
    def _():
        pltpu.sync_copy(tile_at(back, me), arrived.at[me])

    @pl.loop(0, side // SLICE)
    def _(i):
        keep(pl.ds(pl.multiple_of(i * SLICE, SLICE), SLICE))

    def flip_grad(rows):
        flip[rows, :] = grad[:, rows].T

    chunked(flip_grad)

    def grams(rows):
        lgram_new[rows, :] = (
            gram_decay * lgram[rows, :].astype(jnp.float32)
            + (1.0 - gram_decay) * nt(grad[rows, :], grad[...])
        ).astype(jnp.bfloat16)
        rgram_new[rows, :] = (
            gram_decay * rgram[rows, :].astype(jnp.float32)
            + (1.0 - gram_decay) * nt(flip[rows, :], flip[...])
        ).astype(jnp.bfloat16)

    chunked(grams)

    @pl.when(owner)
    def _():
        wait_tiles(arrived, 111, grad_send)
        wait_tiles(arrived, 127, back_send)
        wait_tiles(arrived, 111, back_recv)

    @pl.when(jnp.logical_not(owner))
    def _():
        wait_tiles(arrived, 112, grad_send)
        wait_tiles(arrived, 112, back_recv)


def wait_tiles(ref, tiles, sem):
    part = ref.at[pl.ds(0, tiles)]
    pltpu.make_async_copy(part, part, sem).wait()


def publish(slots, arrived, *refs):
    kept, update, made, tile_sem, sems = refs[:4], refs[4], refs[5:9], refs[9], refs[10]
    copies = [
        pltpu.make_async_copy(a, b, sems.at[n]) for n, (a, b) in enumerate(zip(kept, made))
    ]
    for copy in copies:
        copy.start()

    @pl.loop(0, update.shape[0])
    def _(b):
        pltpu.make_async_copy(arrived.at[slots[b]], update.at[b], tile_sem).start()

    every = arrived.at[pl.ds(0, update.shape[0])]
    pltpu.make_async_copy(every, update, tile_sem).wait()
    for copy in copies:
        copy.wait()


def on_device(
    grad_codes,
    grad_scales,
    block_slot,
    left_basis,
    right_basis,
    first_moment,
    second_moment,
    left_gram,
    right_gram,
):
    block_rows, tile_rows, block_cols, tile_cols = grad_codes.shape
    blocks = block_rows * block_cols
    side = left_basis.shape[1]
    bf16 = jnp.bfloat16
    codes = grad_codes.transpose(0, 2, 1, 3).reshape(blocks, tile_rows, tile_cols)
    scales = grad_scales.transpose(2, 3, 0, 1).reshape(blocks, tile_rows)
    held = [
        pltpu.with_memory_space_constraint(a, pltpu.HBM)
        for a in (
            block_slot.reshape(1, blocks),
            codes,
            scales,
            left_basis[0],
            right_basis[0],
            first_moment[0],
            second_moment[0],
            left_gram[0],
            right_gram[0],
        )
    ]
    square = (side, side)
    anywhere = pl.BlockSpec(memory_space=pltpu.HBM)
    outs = pl.pallas_call(
        kernel,
        name="soap_exchange",
        out_shape=[pltpu.VMEM((128, tile_rows, tile_cols), bf16)]
        + [pltpu.VMEM(square, bf16)] * 4,
        in_specs=[anywhere] * 9,
        out_specs=[pl.BlockSpec(memory_space=pltpu.VMEM)] * 5,
        scratch_shapes=[
            pltpu.VMEM((1, blocks), jnp.int32),
            pltpu.VMEM((blocks, tile_rows), bf16),
            pltpu.VMEM((1, blocks), jnp.int32),
            pltpu.SMEM((1, blocks), jnp.int32),
            pltpu.VMEM((blocks, tile_rows, tile_cols), bf16),
            pltpu.VMEM((blocks, tile_rows, tile_cols), bf16),
        ]
        + [pltpu.VMEM(square, bf16)] * 12
        + [
            pltpu.VMEM(square, jnp.float32),
            pltpu.VMEM((PART, side), jnp.float32),
            pltpu.VMEM((PART, side), jnp.float32),
            pltpu.VMEM((CHUNK, side), bf16),
            pltpu.SemaphoreType.DMA((9,)),
            pltpu.SemaphoreType.DMA,
            pltpu.SemaphoreType.DMA,
            pltpu.SemaphoreType.DMA((2,)),
            pltpu.SemaphoreType.DMA,
            pltpu.SemaphoreType.DMA,
        ],
        compiler_params=pltpu.CompilerParams(
            collective_id=0, has_side_effects=True, vmem_limit_bytes=40 << 20
        ),
    )(*held)
    outs = pl.pallas_call(
        publish,
        name="publish",
        out_shape=[jax.ShapeDtypeStruct(codes.shape, bf16)]
        + [jax.ShapeDtypeStruct(square, bf16)] * 4,
        in_specs=[pl.BlockSpec(memory_space=pltpu.SMEM)]
        + [pl.BlockSpec(memory_space=pltpu.VMEM)] * 5,
        out_specs=[pl.BlockSpec(memory_space=pltpu.HBM)] * 5,
        scratch_shapes=[pltpu.SemaphoreType.DMA, pltpu.SemaphoreType.DMA((4,))],
        compiler_params=pltpu.CompilerParams(vmem_limit_bytes=1 << 20),
    )(block_slot, *[pltpu.with_memory_space_constraint(a, pltpu.VMEM) for a in outs])
    update = outs[0].reshape(block_rows, block_cols, tile_rows, tile_cols)
    return (update.transpose(0, 2, 1, 3),) + tuple(a[None] for a in outs[1:])


def solution(mesh):
    whole = P(("dp", "tensor"), None, None)
    tiles = P(None, "tensor", None, "dp")
    return jax.shard_map(
        on_device,
        mesh=mesh,
        in_specs=(tiles, tiles, P()) + (whole,) * 6,
        out_specs=(tiles,) + (whole,) * 4,
        check_vma=False,
    )
```

```python
import functools

import jax
import jax.numpy as jnp
from jax import lax
from jax.experimental import pallas as pl
from jax.experimental.pallas import tpu as pltpu
from jax.sharding import PartitionSpec as P

beta_first = 0.9
beta_second = 0.95
gram_decay = 0.9
epsilon = 1e-08

CHUNK = 256
SLICE = 16
PART = 128


def nt(a, b):
    return lax.dot_general(a, b, (((1,), (1,)), ((), ())), preferred_element_type=jnp.float32)


def nn(a, b):
    return jnp.dot(a, b, preferred_element_type=jnp.float32)


def digits(i, *sizes):
    out = []
    for n in sizes:
        out.append(lax.rem(i, n))
        i = i // n
    return out


def kernel(
    slots_hbm,
    codes_hbm,
    scales_hbm,
    left_hbm,
    right_hbm,
    first_hbm,
    second_hbm,
    lgram_hbm,
    rgram_hbm,
    arrived,
    first_new,
    second_new,
    lgram_new,
    rgram_new,
    slots,
    scales,
    table,
    inverse,
    codes,
    stage,
    grad,
    flip,
    left,
    left_t,
    right,
    first,
    second,
    lgram,
    rgram,
    half,
    direction,
    back,
    rotated,
    turned_even,
    turned_odd,
    half_back,
    load_sem,
    table_sem,
    grad_send,
    grad_recv,
    back_send,
    back_recv,
):
    blocks, tile_rows, tile_cols = codes.shape
    side = grad.shape[0]
    dp_index = lax.axis_index("dp")
    t_index = lax.axis_index("tensor")
    z, c = dp_index // 2, lax.rem(dp_index, 2)
    x, y = t_index // 4, lax.rem(t_index, 4)
    me = dp_index * 16 + t_index
    owner = me < blocks

    loads = [
        pltpu.make_async_copy(src, dst, load_sem.at[n])
        for n, (src, dst) in enumerate(
            (
                (slots_hbm, slots),
                (scales_hbm, scales),
                (codes_hbm, codes),
                (left_hbm, left),
                (right_hbm, right),
                (first_hbm, first),
                (second_hbm, second),
                (lgram_hbm, lgram),
                (rgram_hbm, rgram),
            )
        )
    ]
    for copy in loads[:3]:
        copy.start()

    barrier = pltpu.get_barrier_semaphore()

    def greet(i):
        o = lax.rem(me + i, 128)
        pl.semaphore_signal(
            barrier, inc=1, device_id={"dp": o // 16, "tensor": lax.rem(o, 16)}
        )

    @pl.loop(0, 18)
    def _(i):
        for q in range(7):
            greet(1 + 7 * i + q)

    greet(127)

    loads[0].wait()
    down = lax.broadcasted_iota(jnp.int32, (blocks, blocks), 0)
    across = lax.broadcasted_iota(jnp.int32, (blocks, blocks), 1)
    column = jnp.sum(jnp.where(down == across, slots[...], 0), axis=1, keepdims=True)
    table[...] = jnp.max(jnp.where(column == across, down, 0), axis=0, keepdims=True)
    fetch = pltpu.make_async_copy(table, inverse, table_sem)
    fetch.start()

    loads[1].wait()
    eye = (
        lax.broadcasted_iota(jnp.int32, (tile_rows, tile_rows), 0)
        == lax.broadcasted_iota(jnp.int32, (tile_rows, tile_rows), 1)
    ).astype(jnp.bfloat16)
    scale_t = nt(eye, scales[...])
    lane = lax.broadcasted_iota(jnp.int32, (tile_rows, blocks), 1)
    lane_block = lax.rem(lane, 8) * 14 + lane // 8

    def tile_at(ref, o):
        rows = pl.multiple_of(lax.rem(o, 16) * tile_rows, tile_rows)
        cols = pl.multiple_of((o // 16) * tile_cols, tile_cols)
        return ref.at[pl.ds(rows, tile_rows), pl.ds(cols, tile_cols)]

    fetch.wait()
    loads[2].wait()
    for copy in loads[3:]:
        copy.start()

    @pl.loop(0, blocks // 4)
    def _(i):
        for q in range(4):
            o = 4 * i + q
            block = inverse[0, o]
            scale = jnp.sum(
                jnp.where(lane_block == block, scale_t, 0.0), axis=1, keepdims=True
            )
            stage[o] = (codes[block].astype(jnp.float32) * scale).astype(jnp.bfloat16)

    pl.semaphore_wait(barrier, 127)

    @pl.loop(0, 128)
    def _(i):
        dzb, a, b, zp, core = digits(i, 2, 4, 4, 2, 2)
        z2 = lax.rem(z + 2 * dzb + 1 - zp, 4)
        x2 = lax.rem(x + a, 4)
        y2 = lax.rem(y + a + b, 4)
        o = (z2 * 2 + core) * 16 + x2 * 4 + y2

        @pl.when(jnp.logical_and(o < blocks, o != me))
        def _():
            pltpu.make_async_remote_copy(
                stage.at[o],
                tile_at(grad, me),
                grad_send,
                grad_recv.at[zp],
                device_id={"dp": z2 * 2 + core, "tensor": x2 * 4 + y2},
            ).start()

    @pl.when(owner)
    def _():
        pltpu.sync_copy(stage.at[me], tile_at(grad, me))

    @pl.when(jnp.logical_not(owner))
    def _():
        grad[...] = jnp.zeros_like(grad)

    def chunked(body):
        @pl.loop(0, side // CHUNK)
        def _(i):
            body(pl.ds(pl.multiple_of(i * CHUNK, CHUNK), CHUNK))

    loads[3].wait()

    def flip_left(rows):
        left_t[rows, :] = left[:, rows].T

    chunked(flip_left)
    for copy in loads[4:]:
        copy.wait()

    def span(k):
        return pl.ds(pl.multiple_of(lax.rem(z + k, 4) * CHUNK, CHUNK), CHUNK)

    def to_half(k):
        half[:, span(k)] = nn(left_t[...], grad[:, span(k)]).astype(jnp.bfloat16)

    def turn(rows, k):
        return nn(half[rows, span(k)], right[span(k), :])

    @pl.when(owner)
    def _():
        wait_tiles(arrived, 64, grad_recv.at[0])

    to_half(1)
    to_half(3)

    def turn_first(rows):
        rotated[rows, :] = turn(rows, 1) + turn(rows, 3)

    chunked(turn_first)

    @pl.when(owner)
    def _():
        wait_tiles(arrived, 63, grad_recv.at[1])

    to_half(2)
    to_half(0)

    def step(rows, turned):
        m = beta_first * first[rows, :].astype(jnp.float32) + (1.0 - beta_first) * turned
        v = (
            beta_second * second[rows, :].astype(jnp.float32)
            + (1.0 - beta_second) * turned * turned
        )
        root = v * lax.rsqrt(v) + epsilon
        direction[rows, :] = (m * lax.rsqrt(root * root)).astype(jnp.bfloat16)

    def keep(rows):
        turned = rotated[rows, :]
        m = beta_first * first[rows, :].astype(jnp.float32) + (1.0 - beta_first) * turned
        v = (
            beta_second * second[rows, :].astype(jnp.float32)
            + (1.0 - beta_second) * turned * turned
        )
        first_new[rows, :] = m.astype(jnp.bfloat16)
        second_new[rows, :] = v.astype(jnp.bfloat16)

    parts = side // PART
    for i in range(parts + 1):
        if i < parts:
            rows = pl.ds(i * PART, PART)
            rotated[rows, :] = rotated[rows, :] + turn(rows, 2) + turn(rows, 0)
        if i > 0:
            for j in range(PART // SLICE):
                step(
                    pl.ds((i - 1) * PART + j * SLICE, SLICE),
                    rotated[pl.ds((i - 1) * PART + j * SLICE, SLICE), :],
                )

    @pl.loop(0, 8)
    def _(turn_at):
        dyb, yp, even = digits(turn_at, 2, 2, 2)
        places = [
            pl.multiple_of(
                lax.rem(x + 2 * k + 1 - even, 4) * CHUNK
                + lax.rem(y + 2 * dyb + yp, 4) * tile_rows,
                tile_rows,
            )
            for k in range(2)
        ]
        picked = [left[pl.ds(p, tile_rows), :] for p in places]
        half_back[...] = nn(jnp.concatenate(picked, axis=0), direction[...]).astype(
            jnp.bfloat16
        )
        out = nt(half_back[...], right[...]).astype(jnp.bfloat16)
        for n, p in enumerate(places):
            back[pl.ds(p, tile_rows), :] = out[n * tile_rows : (n + 1) * tile_rows]

        @pl.when(owner)
        def _():
            @pl.loop(0, 16)
            def _(i):
                core, dzb, k, zp = digits(i, 2, 2, 2, 2)
                core = lax.rem(core + c, 2)
                z2 = lax.rem(z + 2 * (dzb + c) + 1 - zp, 4)
                x2 = lax.rem(x + 2 * k + 1 - even, 4)
                y2 = lax.rem(y + 2 * dyb + yp, 4)
                o = (z2 * 2 + core) * 16 + x2 * 4 + y2

                @pl.when(o != me)
                def _():
                    pltpu.make_async_remote_copy(
                        tile_at(back, o),
                        arrived.at[me],
                        back_send,
                        back_recv,
                        device_id={"dp": z2 * 2 + core, "tensor": x2 * 4 + y2},
                    ).start()

    @pl.when(owner)
    def _():
        pltpu.sync_copy(tile_at(back, me), arrived.at[me])

    @pl.loop(0, side // SLICE)
    def _(i):
        keep(pl.ds(pl.multiple_of(i * SLICE, SLICE), SLICE))

    def flip_grad(rows):
        flip[rows, :] = grad[:, rows].T

    chunked(flip_grad)

    def grams(rows):
        lgram_new[rows, :] = (
            gram_decay * lgram[rows, :].astype(jnp.float32)
            + (1.0 - gram_decay) * nt(grad[rows, :], grad[...])
        ).astype(jnp.bfloat16)
        rgram_new[rows, :] = (
            gram_decay * rgram[rows, :].astype(jnp.float32)
            + (1.0 - gram_decay) * nt(flip[rows, :], flip[...])
        ).astype(jnp.bfloat16)

    chunked(grams)

    @pl.when(owner)
    def _():
        wait_tiles(arrived, 111, grad_send)
        wait_tiles(arrived, 127, back_send)
        wait_tiles(arrived, 111, back_recv)

    @pl.when(jnp.logical_not(owner))
    def _():
        wait_tiles(arrived, 112, grad_send)
        wait_tiles(arrived, 112, back_recv)


def wait_tiles(ref, tiles, sem):
    part = ref.at[pl.ds(0, tiles)]
    pltpu.make_async_copy(part, part, sem).wait()


def publish(slots, arrived, *refs):
    kept, update, made, tile_sem, sems = refs[:4], refs[4], refs[5:9], refs[9], refs[10]
    copies = [
        pltpu.make_async_copy(a, b, sems.at[n]) for n, (a, b) in enumerate(zip(kept, made))
    ]
    for copy in copies:
        copy.start()

    @pl.loop(0, update.shape[0])
    def _(b):
        pltpu.make_async_copy(arrived.at[slots[b]], update.at[b], tile_sem).start()

    every = arrived.at[pl.ds(0, update.shape[0])]
    pltpu.make_async_copy(every, update, tile_sem).wait()
    for copy in copies:
        copy.wait()


def on_device(
    grad_codes,
    grad_scales,
    block_slot,
    left_basis,
    right_basis,
    first_moment,
    second_moment,
    left_gram,
    right_gram,
):
    block_rows, tile_rows, block_cols, tile_cols = grad_codes.shape
    blocks = block_rows * block_cols
    side = left_basis.shape[1]
    bf16 = jnp.bfloat16
    codes = grad_codes.transpose(0, 2, 1, 3).reshape(blocks, tile_rows, tile_cols)
    scales = grad_scales.transpose(2, 3, 0, 1).reshape(blocks, tile_rows)
    held = [
        pltpu.with_memory_space_constraint(a, pltpu.HBM)
        for a in (
            block_slot.reshape(1, blocks),
            codes,
            scales,
            left_basis[0],
            right_basis[0],
            first_moment[0],
            second_moment[0],
            left_gram[0],
            right_gram[0],
        )
    ]
    square = (side, side)
    anywhere = pl.BlockSpec(memory_space=pltpu.HBM)
    outs = pl.pallas_call(
        kernel,
        name="soap_exchange",
        out_shape=[pltpu.VMEM((128, tile_rows, tile_cols), bf16)]
        + [pltpu.VMEM(square, bf16)] * 4,
        in_specs=[anywhere] * 9,
        out_specs=[pl.BlockSpec(memory_space=pltpu.VMEM)] * 5,
        scratch_shapes=[
            pltpu.VMEM((1, blocks), jnp.int32),
            pltpu.VMEM((blocks, tile_rows), bf16),
            pltpu.VMEM((1, blocks), jnp.int32),
            pltpu.SMEM((1, blocks), jnp.int32),
            pltpu.VMEM((blocks, tile_rows, tile_cols), bf16),
            pltpu.VMEM((blocks, tile_rows, tile_cols), bf16),
        ]
        + [pltpu.VMEM(square, bf16)] * 12
        + [
            pltpu.VMEM(square, jnp.float32),
            pltpu.VMEM((PART, side), jnp.float32),
            pltpu.VMEM((PART, side), jnp.float32),
            pltpu.VMEM((PART, side), bf16),
            pltpu.SemaphoreType.DMA((9,)),
            pltpu.SemaphoreType.DMA,
            pltpu.SemaphoreType.DMA,
            pltpu.SemaphoreType.DMA((2,)),
            pltpu.SemaphoreType.DMA,
            pltpu.SemaphoreType.DMA,
        ],
        compiler_params=pltpu.CompilerParams(
            collective_id=0, has_side_effects=True, vmem_limit_bytes=40 << 20
        ),
    )(*held)
    outs = pl.pallas_call(
        publish,
        name="publish",
        out_shape=[jax.ShapeDtypeStruct(codes.shape, bf16)]
        + [jax.ShapeDtypeStruct(square, bf16)] * 4,
        in_specs=[pl.BlockSpec(memory_space=pltpu.SMEM)]
        + [pl.BlockSpec(memory_space=pltpu.VMEM)] * 5,
        out_specs=[pl.BlockSpec(memory_space=pltpu.HBM)] * 5,
        scratch_shapes=[pltpu.SemaphoreType.DMA, pltpu.SemaphoreType.DMA((4,))],
        compiler_params=pltpu.CompilerParams(vmem_limit_bytes=1 << 20),
    )(block_slot, *[pltpu.with_memory_space_constraint(a, pltpu.VMEM) for a in outs])
    update = outs[0].reshape(block_rows, block_cols, tile_rows, tile_cols)
    return (update.transpose(0, 2, 1, 3),) + tuple(a[None] for a in outs[1:])


def solution(mesh):
    whole = P(("dp", "tensor"), None, None)
    tiles = P(None, "tensor", None, "dp")
    return jax.shard_map(
        on_device,
        mesh=mesh,
        in_specs=(tiles, tiles, P()) + (whole,) * 6,
        out_specs=(tiles,) + (whole,) * 4,
        check_vma=False,
    )
```
